32 devices in a mesh: dp: 16 (over z, y, core), tensor: 2 (over x).
Axes of the slice: x: 2, y: 2, z: 4, core: 2. Of those that a mesh axis runs over, the one named last changes fastest.
Arguments:
- latent_in: bfloat16 [32, 512, 1408], P('dp', 'tensor'), may hold values from -6 to 6
- skip_in: bfloat16 [32, 512, 1408], P('dp', 'tensor'), may hold values from -6 to 6
- condition: bfloat16 [32, 1408], P('dp'), may hold values from -6 to 6
- text_states: bfloat16 [32, 128, 1024], P('dp', None, 'tensor'), may hold values from -6 to 6
- positions: int32 [32, 2, 512], P('dp'), may hold values from 0 to 63, as said below
- out_cotangent: bfloat16 [32, 512, 1408], P('dp', 'tensor'), may hold values from -6 to 6
- w_skip: bfloat16 [2816, 1408], P('dp', 'tensor'), may hold values from -0.109375 to 0.109375
- w_ada: bfloat16 [1408, 1408], P('dp'), may hold values from -0.15625 to 0.15625
- w_qkv: bfloat16 [3, 1408, 1408], P(None, 'dp', 'tensor'), may hold values from -0.15625 to 0.15625
- w_out: bfloat16 [1408, 1408], P('tensor', 'dp'), may hold values from -2.5 to 2.5
- w_cq: bfloat16 [1408, 1408], P('dp', 'tensor'), may hold values from -0.15625 to 0.15625
- w_ckv: bfloat16 [2, 1024, 1408], P(None, 'dp', 'tensor'), may hold values from -0.1875 to 0.1875
- w_co: bfloat16 [1408, 1408], P('tensor', 'dp'), may hold values from -1.75 to 1.75
- w_up: bfloat16 [1408, 6144], P('dp', 'tensor'), may hold values from -0.15625 to 0.15625
- w_down: bfloat16 [6144, 1408], P('tensor', 'dp'), may hold values from -0.078125 to 0.078125
- g_skip: float32 [1408], replicated, may hold values from 0.1 to 1.9
- g_self: float32 [1408], replicated, may hold values from 0.1 to 1.9
- g_cross: float32 [1408], replicated, may hold values from 0.1 to 1.9
- g_mlp: float32 [1408], replicated, may hold values from 0.1 to 1.9
- g_q: float32 [88], replicated, may hold values from 0.1 to 1.9
- g_k: float32 [88], replicated, may hold values from 0.1 to 1.9
- g_cq: float32 [88], replicated, may hold values from 0.1 to 1.9
- g_ck: float32 [88], replicated, may hold values from 0.1 to 1.9
Outputs:
- block_out: bfloat16 [32, 512, 1408], P('dp', 'tensor')
- grad_x: float32 [32, 512, 1408], P('dp', 'tensor')
- grad_skip: float32 [32, 512, 1408], P('dp', 'tensor')
- grad_text: float32 [32, 128, 1024], P('dp', None, 'tensor')
- grad_w_skip: float32 [2816, 1408], P('dp', 'tensor')
- grad_w_ada: float32 [1408, 1408], P('dp')
- grad_w_qkv: float32 [3, 1408, 1408], P(None, 'dp', 'tensor')
- grad_w_out: float32 [1408, 1408], P('tensor', 'dp')
- grad_w_cq: float32 [1408, 1408], P('dp', 'tensor')
- grad_w_ckv: float32 [2, 1024, 1408], P(None, 'dp', 'tensor')
- grad_w_co: float32 [1408, 1408], P('tensor', 'dp')
- grad_w_up: float32 [1408, 6144], P('dp', 'tensor')
- grad_w_down: float32 [6144, 1408], P('tensor', 'dp')
- grad_g_skip: float32 [1408], replicated
- grad_g_self: float32 [1408], replicated
- grad_g_cross: float32 [1408], replicated
- grad_g_mlp: float32 [1408], replicated
- grad_g_q: float32 [88], replicated
- grad_g_k: float32 [88], replicated
- grad_g_cq: float32 [88], replicated
- grad_g_ck: float32 [88], replicated
The draws below stay inside these ranges and needn't reach their ends.
Inputs may be any that keep to these rules, and one draw needn't show every extreme that they name: `positions`: for each latent a grid width W of 16, 32 or 64 that divides 512; token t sits at row t // W and column t % W (first row, then column).
All inputs are finite; a program needn't handle non-finite values.
Results may differ from the reference program's by a relative error of at most 0.025.
Values may be sent and summed in bfloat16 or wider, within the bound.
A program may use at most 184 MiB of HBM per device.

```python
import jax
import jax.numpy as jnp
from jax import lax

D = 1408
HD = 88
FF = 6144
E = 1024
TXT = 128
SEQ = 512
LATENTS = 32


def draw_positions(key, part):
    choose = jax.random.randint(key, (LATENTS,), 0, 3)
    choose = choose.at[0].set(0).at[1].set(2)
    grid_width = jnp.left_shift(jnp.full((LATENTS,), 16, jnp.int32), choose.astype(jnp.int32))
    token_ids = jnp.arange(SEQ, dtype=jnp.int32)
    row_ids = token_ids[None, :] // grid_width[:, None]
    col_ids = token_ids[None, :] % grid_width[:, None]
    return jnp.stack([row_ids, col_ids], 1).astype(jnp.int32)


def levels(key, shape, pieces, low, top_value):
    gain = 1.0
    for dim, parts in pieces:
        heights = jax.random.uniform(jax.random.fold_in(jax.random.fold_in(key, 6), dim), (parts,), jnp.float32, low / len(pieces), top_value / len(pieces))
        gain = gain * jnp.repeat(jnp.exp(heights), shape[dim] // parts).reshape((-1,) + (1,) * (len(shape) - 1 - dim))
    return gain


def noise(key, extent, deviation, reach, cuts=(), held_as=jnp.bfloat16):
    values = jax.random.normal(key, extent, jnp.float32) * deviation
    if len(cuts) > 0:
        values = levels(key, extent, cuts, -0.22, 0.18) * values
    return jnp.clip(values, min=-reach, max=reach).astype(held_as)


def setup_inputs(seed: int = 0) -> dict:
    key_list = jax.random.split(jax.random.key(seed), 24)
    latent_in = noise(key_list[0], (LATENTS, SEQ, D), 1.0, 6.0, ((0, 16), (1, 2)))
    skip_in = noise(key_list[1], (LATENTS, SEQ, D), 1.0, 6.0, ((0, 16), (1, 2)))
    condition = noise(key_list[2], (LATENTS, D), 1.0, 6.0, ((0, 16),))
    text_states = noise(key_list[3], (LATENTS, TXT, E), 1.0, 6.0, ((0, 16), (2, 2)))
    positions = draw_positions(jax.random.fold_in(key_list[23], 71), 0)
    out_cotangent = noise(key_list[5], (LATENTS, SEQ, D), 1.0, 6.0, ((0, 16), (1, 2)))
    w_skip = noise(key_list[6], (2 * D, D), (2 * D) ** -0.5, 0.109375, ((0, 16), (1, 2)))
    w_ada = noise(key_list[7], (D, D), D ** -0.5, 0.15625, ((0, 16),))
    w_qkv = noise(key_list[8], (3, D, D), D ** -0.5, 0.15625, ((1, 16), (2, 2)))
    w_out = noise(key_list[9], (D, D), (max(D // 256, 4)) ** -0.5, 2.5, ((0, 2), (1, 16)))
    w_cq = noise(key_list[10], (D, D), D ** -0.5, 0.15625, ((0, 16), (1, 2)))
    w_ckv = noise(key_list[11], (2, E, D), E ** -0.5, 0.1875, ((1, 16), (2, 2)))
    w_co = noise(key_list[12], (D, D), (max(D // 128, 4)) ** -0.5, 1.75, ((0, 2), (1, 16)))
    w_up = noise(key_list[13], (D, FF), D ** -0.5, 0.15625, ((0, 16), (1, 2)))
    w_down = noise(key_list[14], (FF, D), FF ** -0.5, 0.078125, ((0, 2), (1, 16)))
    g_skip = jnp.clip(1.0 + 0.18 * jax.random.normal(key_list[15], (D,), jnp.float32), 0.1, 1.9)
    g_self = jnp.clip(1.0 + 0.18 * jax.random.normal(key_list[16], (D,), jnp.float32), 0.1, 1.9)
    g_cross = jnp.clip(1.0 + 0.18 * jax.random.normal(key_list[17], (D,), jnp.float32), 0.1, 1.9)
    g_mlp = jnp.clip(1.0 + 0.18 * jax.random.normal(key_list[18], (D,), jnp.float32), 0.1, 1.9)
    g_q = jnp.clip(1.0 + 0.18 * jax.random.normal(key_list[19], (HD,), jnp.float32), 0.1, 1.9)
    g_k = jnp.clip(1.0 + 0.18 * jax.random.normal(key_list[20], (HD,), jnp.float32), 0.1, 1.9)
    g_cq = jnp.clip(1.0 + 0.18 * jax.random.normal(key_list[21], (HD,), jnp.float32), 0.1, 1.9)
    g_ck = jnp.clip(1.0 + 0.18 * jax.random.normal(key_list[22], (HD,), jnp.float32), 0.1, 1.9)
    return dict(latent_in=latent_in, skip_in=skip_in, condition=condition, text_states=text_states, positions=positions, out_cotangent=out_cotangent, w_skip=w_skip, w_ada=w_ada, w_qkv=w_qkv, w_out=w_out, w_cq=w_cq, w_ckv=w_ckv, w_co=w_co, w_up=w_up, w_down=w_down, g_skip=g_skip, g_self=g_self, g_cross=g_cross, g_mlp=g_mlp, g_q=g_q, g_k=g_k, g_cq=g_cq, g_ck=g_ck)


EPSILON = 1e-06
HIGH = lax.Precision.HIGHEST

@jax.custom_vjp
def low(v):
    return lax.optimization_barrier(v.astype(jnp.bfloat16)).astype(jnp.float32)

@jax.custom_vjp
def low_back(v):
    return v

def low_keep(v):
    return (low(v), None)

def low_pass(kept, grad):
    return (grad,)

def back_keep(v):
    return (v, None)

def back_low(kept, grad):
    return (low(grad),)
low.defvjp(low_keep, low_pass)
low_back.defvjp(back_keep, back_low)

def layer_norm(values_in, gain_vec):
    center_mean = lax.optimization_barrier(jnp.mean(values_in, -1, keepdims=True))
    centered = values_in - center_mean
    variance = lax.optimization_barrier(jnp.mean(centered * centered, -1, keepdims=True))
    return centered * lax.rsqrt(variance + EPSILON) * gain_vec

def rotate_half(values_in):
    quarter = values_in.shape[-1] // 4
    return jnp.concatenate([-values_in[..., quarter:2 * quarter], values_in[..., :quarter], -values_in[..., 3 * quarter:], values_in[..., 2 * quarter:3 * quarter]], -1)

def rope_tables(places, head_size):
    quarter = head_size // 4
    frequencies = 10000.0 ** (-jnp.arange(quarter, dtype=jnp.float32) / quarter)
    row_angle = places[0].astype(jnp.float32)[:, None] * frequencies[None, :]
    col_angle = places[1].astype(jnp.float32)[:, None] * frequencies[None, :]
    cosine = jnp.concatenate([jnp.cos(row_angle), jnp.cos(row_angle), jnp.cos(col_angle), jnp.cos(col_angle)], -1)
    sine_tab = jnp.concatenate([jnp.sin(row_angle), jnp.sin(row_angle), jnp.sin(col_angle), jnp.sin(col_angle)], -1)
    return (cosine, sine_tab)

def apply_rope(values_in, cosine, sine_tab):
    return values_in * cosine[:, None, :] + rotate_half(values_in) * sine_tab[:, None, :]

def matmul_high(left_side, right_side):
    return jnp.dot(left_side, right_side, precision=HIGH)

def split_heads(flat_in, head_size):
    return flat_in.reshape(flat_in.shape[0], -1, head_size)

def attention(queries, key_vecs, values, scale_factor):
    seq_rows = queries.shape[0]
    block_rows = min(512, seq_rows)
    query_blocks = queries.reshape(seq_rows // block_rows, block_rows, queries.shape[1], queries.shape[2])

    def one_block(query_block):
        scores = low_back(jnp.einsum('qhd,khd->hqk', query_block, key_vecs, precision=HIGH) * scale_factor)
        weights = jax.nn.softmax(scores, -1)
        mixed_out = jnp.einsum('hqk,khd->qhd', low(weights), values, precision=HIGH)
        return low_back(low(mixed_out))
    mixed_blocks = lax.map(jax.checkpoint(one_block), query_blocks)
    return mixed_blocks.reshape(queries.shape)

def forward(weight_set, gain_set, latent_val, skip_val, text_val, silu_cond, cosine, sine_tab):
    w_skip, w_ada, w_qkv, w_out, w_cq, w_ckv, w_co, w_up, w_down = weight_set
    g_skip, g_self, g_cross, g_mlp, g_q, g_k, g_cq, g_ck = gain_set
    head_size = g_q.shape[0]
    scale_factor = head_size ** (-0.5)
    joined = jnp.concatenate([latent_val, skip_val], -1)
    first_out = low_back(low(matmul_high(joined, w_skip)))
    resid_one = layer_norm(first_out, g_skip)
    shift_vec = matmul_high(low(silu_cond)[None, :], w_ada)[0]
    attn_in = low(layer_norm(resid_one, g_self) + shift_vec)
    query_proj = low_back(matmul_high(attn_in, w_qkv[0]))
    key_proj = low_back(matmul_high(attn_in, w_qkv[1]))
    value_proj = low_back(low(matmul_high(attn_in, w_qkv[2])))
    queries = low(apply_rope(layer_norm(split_heads(query_proj, head_size), g_q), cosine, sine_tab))
    key_vecs = low(apply_rope(layer_norm(split_heads(key_proj, head_size), g_k), cosine, sine_tab))
    mixed_out = attention(queries, key_vecs, split_heads(value_proj, head_size), scale_factor)
    resid_two = resid_one + low_back(matmul_high(mixed_out.reshape(mixed_out.shape[0], -1), w_out))
    cross_in = low(layer_norm(resid_two, g_cross))
    cross_queries = low(apply_rope(layer_norm(split_heads(low_back(matmul_high(cross_in, w_cq)), head_size), g_cq), cosine, sine_tab))
    cross_keys = low(layer_norm(split_heads(low_back(matmul_high(text_val, w_ckv[0])), head_size), g_ck))
    cross_values = split_heads(low_back(low(matmul_high(text_val, w_ckv[1]))), head_size)
    cross_mixed = attention(cross_queries, cross_keys, cross_values, scale_factor)
    resid_three = resid_two + low_back(matmul_high(cross_mixed.reshape(cross_mixed.shape[0], -1), w_co))
    mlp_in = low(layer_norm(resid_three, g_mlp))
    inner_pre = low_back(matmul_high(mlp_in, w_up))
    hidden = low_back(low(jax.nn.gelu(inner_pre, approximate=True)))
    return resid_three + low_back(matmul_high(hidden, w_down))

def reference(latent_in, skip_in, condition, text_states, positions, out_cotangent, w_skip, w_ada, w_qkv, w_out, w_cq, w_ckv, w_co, w_up, w_down, g_skip, g_self, g_cross, g_mlp, g_q, g_k, g_cq, g_ck):
    weight_set = tuple((array_in.astype(jnp.float32) for array_in in (w_skip, w_ada, w_qkv, w_out, w_cq, w_ckv, w_co, w_up, w_down)))
    gain_set = tuple((array_in.astype(jnp.float32) for array_in in (g_skip, g_self, g_cross, g_mlp, g_q, g_k, g_cq, g_ck)))
    head_size = g_q.shape[0]

    def per_latent(totals, inputs):
        latent_one, skip_one, cond_one, text_one, places, grad_one = inputs
        cosine, sine_tab = rope_tables(places, head_size)
        silu_cond = jax.nn.silu(cond_one.astype(jnp.float32))

        def wrapped(weights_in, gains_in, latent_val, skip_val, text_val):
            return forward(weights_in, gains_in, latent_val, skip_val, text_val, silu_cond, cosine, sine_tab)
        output, pull_back = jax.vjp(wrapped, weight_set, gain_set, latent_one.astype(jnp.float32), skip_one.astype(jnp.float32), text_one.astype(jnp.float32))
        grad_weights, grad_gains, grad_x_one, grad_skip_one, grad_text_one = pull_back(grad_one.astype(jnp.float32))
        totals = jax.tree.map(jnp.add, totals, (grad_weights, grad_gains))
        return (totals, (output.astype(jnp.bfloat16), grad_x_one, grad_skip_one, grad_text_one))
    zero_sets = jax.tree.map(jnp.zeros_like, (weight_set, gain_set))
    (grad_weights, grad_gains), (block_out, grad_x, grad_skip, grad_text) = lax.scan(per_latent, zero_sets, (latent_in, skip_in, condition, text_states, positions, out_cotangent))
    return (block_out, grad_x, grad_skip, grad_text, grad_weights[0], grad_weights[1], grad_weights[2], grad_weights[3], grad_weights[4], grad_weights[5], grad_weights[6], grad_weights[7], grad_weights[8], grad_gains[0], grad_gains[1], grad_gains[2], grad_gains[3], grad_gains[4], grad_gains[5], grad_gains[6], grad_gains[7])
```

```python
import jax
import jax.numpy as jnp
from jax import lax
from jax.sharding import PartitionSpec as P

EPSILON = 1e-06
HIGH = lax.Precision.HIGHEST


def multiply(left_side, right_side):
    return jnp.dot(left_side, right_side, preferred_element_type=jnp.float32)


def multiply_left(left_side, right_side):
    return lax.dot_general(
        left_side, right_side, (((0,), (0,)), ((), ())), preferred_element_type=jnp.float32
    )


def multiply_right(left_side, right_side):
    return lax.dot_general(
        left_side, right_side, (((1,), (1,)), ((), ())), preferred_element_type=jnp.float32
    )


def layer_norm(values_in, gain_vec):
    center_mean = jnp.mean(values_in, -1, keepdims=True)
    centered = values_in - center_mean
    variance = jnp.mean(centered * centered, -1, keepdims=True)
    return centered * lax.rsqrt(variance + EPSILON) * gain_vec


def rotate_half(values_in):
    quarter = values_in.shape[-1] // 4
    return jnp.concatenate(
        [
            -values_in[..., quarter : 2 * quarter],
            values_in[..., :quarter],
            -values_in[..., 3 * quarter :],
            values_in[..., 2 * quarter : 3 * quarter],
        ],
        -1,
    )


def rope_tables(places, head_size):
    quarter = head_size // 4
    frequencies = 10000.0 ** (-jnp.arange(quarter, dtype=jnp.float32) / quarter)
    row_angle = places[0].astype(jnp.float32)[:, None] * frequencies[None, :]
    col_angle = places[1].astype(jnp.float32)[:, None] * frequencies[None, :]
    cosine = jnp.concatenate(
        [jnp.cos(row_angle), jnp.cos(row_angle), jnp.cos(col_angle), jnp.cos(col_angle)], -1
    )
    sine_tab = jnp.concatenate(
        [jnp.sin(row_angle), jnp.sin(row_angle), jnp.sin(col_angle), jnp.sin(col_angle)], -1
    )
    return (cosine, sine_tab)


def gelu_tanh(values_in):
    return jax.nn.gelu(values_in, approximate=True)


def gather_rows(values_in):
    return lax.all_gather(values_in, "tensor", axis=0, tiled=True)


def reduce_rows(values_in):
    return lax.psum_scatter(
        values_in.astype(jnp.bfloat16), "tensor", scatter_dimension=0, tiled=True
    ).astype(jnp.float32)


def ada_grad(silu_rows, shift_rows):
    shift_total = lax.psum(shift_rows, "tensor")
    return jnp.einsum("md,me->de", silu_rows.astype(jnp.float32), shift_total, precision=HIGH)


def send_grads(weight_terms, ada_term):
    grad_skip_w, grad_qkv, grad_out_w, grad_cq, grad_ckv, grad_co, grad_up, grad_down = weight_terms
    return (
        lax.psum_scatter(
            grad_skip_w.astype(jnp.bfloat16), "dp", scatter_dimension=0, tiled=True
        ).astype(jnp.float32),
        lax.psum_scatter(
            ada_term.astype(jnp.bfloat16), "dp", scatter_dimension=0, tiled=True
        ).astype(jnp.float32),
        lax.psum_scatter(
            grad_qkv.astype(jnp.bfloat16), "dp", scatter_dimension=1, tiled=True
        ).astype(jnp.float32),
        lax.psum_scatter(
            grad_out_w.astype(jnp.bfloat16), "dp", scatter_dimension=1, tiled=True
        ).astype(jnp.float32),
        lax.psum_scatter(
            grad_cq.astype(jnp.bfloat16), "dp", scatter_dimension=0, tiled=True
        ).astype(jnp.float32),
        lax.psum_scatter(
            grad_ckv.astype(jnp.bfloat16), "dp", scatter_dimension=1, tiled=True
        ).astype(jnp.float32),
        lax.psum_scatter(
            grad_co.astype(jnp.bfloat16), "dp", scatter_dimension=1, tiled=True
        ).astype(jnp.float32),
        lax.psum_scatter(
            grad_up.astype(jnp.bfloat16), "dp", scatter_dimension=0, tiled=True
        ).astype(jnp.float32),
        lax.psum_scatter(
            grad_down.astype(jnp.bfloat16), "dp", scatter_dimension=1, tiled=True
        ).astype(jnp.float32),
    )


def attend(queries, key_vecs, values, scale_factor):
    seq_rows = queries.shape[0]
    block_rows = min(512, seq_rows)
    query_blocks = queries.reshape(
        seq_rows // block_rows, block_rows, queries.shape[1], queries.shape[2]
    )

    def one_block(query_block):
        scores = (
            jnp.einsum("qhd,khd->hqk", query_block, key_vecs, preferred_element_type=jnp.float32)
            * scale_factor
        )
        row_max = jnp.max(scores, -1, keepdims=True)
        weights = jnp.exp(scores - row_max)
        row_total = jnp.sum(weights, -1, keepdims=True)
        probs_low = (weights / row_total).astype(jnp.bfloat16)
        mixed_out = jnp.einsum(
            "hqk,khd->qhd", probs_low, values, preferred_element_type=jnp.float32
        )
        return (mixed_out.astype(jnp.bfloat16), (row_max + jnp.log(row_total))[..., 0])

    mixed_blocks, log_sums = lax.map(one_block, query_blocks)
    return (mixed_blocks.reshape(queries.shape), log_sums)


def attend_back(queries, key_vecs, values, log_sums, grad_mixed, scale_factor):
    seq_rows = queries.shape[0]
    block_rows = min(512, seq_rows)
    block_shape = (seq_rows // block_rows, block_rows, queries.shape[1], queries.shape[2])

    def one_step(carry_in, inputs):
        grad_keys, grad_values = carry_in
        query_block, lse_block, grad_block = inputs
        scores = (
            jnp.einsum("qhd,khd->hqk", query_block, key_vecs, preferred_element_type=jnp.float32)
            * scale_factor
        )
        probs = jnp.exp(scores - lse_block[..., None])
        grad_probs = jnp.einsum(
            "qhd,khd->hqk", grad_block, values, preferred_element_type=jnp.float32
        )
        delta_row = jnp.sum(grad_probs * probs, -1, keepdims=True)
        grad_scores = (probs * (grad_probs - delta_row)).astype(jnp.bfloat16)
        grad_query = (
            jnp.einsum("hqk,khd->qhd", grad_scores, key_vecs, preferred_element_type=jnp.float32)
            * scale_factor
        )
        grad_keys = (
            grad_keys
            + jnp.einsum(
                "hqk,qhd->khd", grad_scores, query_block, preferred_element_type=jnp.float32
            )
            * scale_factor
        )
        grad_values = grad_values + jnp.einsum(
            "hqk,qhd->khd",
            probs.astype(jnp.bfloat16),
            grad_block,
            preferred_element_type=jnp.float32,
        )
        return ((grad_keys, grad_values), grad_query)

    start_grads = (jnp.zeros(key_vecs.shape, jnp.float32), jnp.zeros(values.shape, jnp.float32))
    (grad_keys, grad_values), grad_queries = lax.scan(
        one_step,
        start_grads,
        (queries.reshape(block_shape), log_sums, grad_mixed.reshape(block_shape)),
    )
    return (grad_queries.reshape(queries.shape), grad_keys, grad_values)


def one_latent(gathered, gain_set, latent_part, skip_part, silu_part, text_full, places, grad_top):
    w_skip, w_ada, w_qkv, w_out, w_cq, w_ckv, w_co, w_up, w_down = gathered
    g_skip, g_self, g_cross, g_mlp, g_q, g_k, g_cq, g_ck = gain_set
    head_size = g_q.shape[0]
    scale_factor = head_size ** (-0.5)
    cosine, sine_tab = rope_tables(places, head_size)

    def rotary(flat_in, gain_vec):
        split_in = flat_in.reshape(flat_in.shape[0], -1, head_size)
        normed = layer_norm(split_in, gain_vec)
        return normed * cosine[:, None, :] + rotate_half(normed) * sine_tab[:, None, :]

    def head_norm(flat_in, gain_vec):
        return layer_norm(flat_in.reshape(flat_in.shape[0], -1, head_size), gain_vec)

    joined = jnp.concatenate([latent_part, skip_part], -1)
    joined_full = gather_rows(joined)
    skip_cols = multiply(joined_full, w_skip).astype(jnp.bfloat16)
    first_out = lax.all_to_all(skip_cols, "tensor", split_axis=0, concat_axis=1, tiled=True).astype(
        jnp.float32
    )
    resid_one, pull_skip = jax.vjp(layer_norm, first_out, g_skip)
    shift_vec = multiply(silu_part[None, :], w_ada)[0]
    normed_self, pull_self = jax.vjp(layer_norm, resid_one, g_self)
    attn_in = gather_rows((normed_self + shift_vec).astype(jnp.bfloat16))
    projected = jnp.einsum("sd,tdf->tsf", attn_in, w_qkv, preferred_element_type=jnp.float32)
    query_rot, pull_query = jax.vjp(rotary, projected[0], g_q)
    key_rot, pull_key = jax.vjp(rotary, projected[1], g_k)
    queries = query_rot.astype(jnp.bfloat16)
    key_vecs = key_rot.astype(jnp.bfloat16)
    values = projected[2].astype(jnp.bfloat16).reshape(queries.shape)
    mixed_out, log_sums = attend(queries, key_vecs, values, scale_factor)
    mixed_flat = mixed_out.reshape(mixed_out.shape[0], -1)
    resid_two = resid_one + reduce_rows(multiply(mixed_flat, w_out))
    normed_cross, pull_cross = jax.vjp(layer_norm, resid_two, g_cross)
    cross_in = gather_rows(normed_cross.astype(jnp.bfloat16))
    cross_query_rot, pull_cross_query = jax.vjp(rotary, multiply(cross_in, w_cq), g_cq)
    text_proj = jnp.einsum("me,tef->tmf", text_full, w_ckv, preferred_element_type=jnp.float32)
    cross_key_rot, pull_cross_key = jax.vjp(head_norm, text_proj[0], g_ck)
    cross_queries = cross_query_rot.astype(jnp.bfloat16)
    cross_keys = cross_key_rot.astype(jnp.bfloat16)
    cross_values = text_proj[1].astype(jnp.bfloat16).reshape(cross_keys.shape)
    cross_mixed, cross_sums = attend(cross_queries, cross_keys, cross_values, scale_factor)
    cross_flat = cross_mixed.reshape(cross_mixed.shape[0], -1)
    resid_three = resid_two + reduce_rows(multiply(cross_flat, w_co))
    normed_mlp, pull_mlp = jax.vjp(layer_norm, resid_three, g_mlp)
    mlp_in = gather_rows(normed_mlp.astype(jnp.bfloat16))
    inner_pre = multiply(mlp_in, w_up)
    hidden_val, pull_gelu = jax.vjp(gelu_tanh, inner_pre)
    hidden_low = hidden_val.astype(jnp.bfloat16)
    resid_four = resid_three + reduce_rows(multiply(hidden_low, w_down))
    output = resid_four.astype(jnp.bfloat16)
    grad_four = grad_top.astype(jnp.float32)
    grad_branch = gather_rows(grad_top)
    grad_down = multiply_left(hidden_low, grad_branch)
    grad_hidden = multiply_right(grad_branch, w_down).astype(jnp.bfloat16).astype(jnp.float32)
    (grad_inner,) = pull_gelu(grad_hidden)
    grad_inner_low = grad_inner.astype(jnp.bfloat16)
    grad_up = multiply_left(mlp_in, grad_inner_low)
    back_three, grad_g_mlp = pull_mlp(reduce_rows(multiply_right(grad_inner_low, w_up)))
    grad_three = grad_four + back_three
    grad_cross_out = gather_rows(grad_three.astype(jnp.bfloat16))
    grad_co = multiply_left(cross_flat, grad_cross_out)
    grad_cross_mixed = (
        multiply_right(grad_cross_out, w_co).astype(jnp.bfloat16).reshape(cross_mixed.shape)
    )
    grad_cq_heads, grad_ck_heads, grad_cv_heads = attend_back(
        cross_queries, cross_keys, cross_values, cross_sums, grad_cross_mixed, scale_factor
    )
    grad_cq_flat, grad_g_cq = pull_cross_query(grad_cq_heads)
    grad_ck_flat, grad_g_ck = pull_cross_key(grad_ck_heads)
    grad_cq_low = grad_cq_flat.astype(jnp.bfloat16)
    text_grads_low = jnp.stack([grad_ck_flat, grad_cv_heads.reshape(grad_ck_flat.shape)]).astype(
        jnp.bfloat16
    )
    grad_cq = multiply_left(cross_in, grad_cq_low)
    grad_ckv = jnp.einsum(
        "me,tmf->tef", text_full, text_grads_low, preferred_element_type=jnp.float32
    )
    grad_text_part = jnp.einsum(
        "tmf,tef->me", text_grads_low, w_ckv, preferred_element_type=jnp.float32
    )
    back_two, grad_g_cross = pull_cross(reduce_rows(multiply_right(grad_cq_low, w_cq)))
    grad_two = grad_three + back_two
    grad_self_out = gather_rows(grad_two.astype(jnp.bfloat16))
    grad_out_w = multiply_left(mixed_flat, grad_self_out)
    grad_mixed = multiply_right(grad_self_out, w_out).astype(jnp.bfloat16).reshape(mixed_out.shape)
    grad_q_heads, grad_k_heads, grad_v_heads = attend_back(
        queries, key_vecs, values, log_sums, grad_mixed, scale_factor
    )
    grad_q_flat, grad_g_q = pull_query(grad_q_heads)
    grad_k_flat, grad_g_k = pull_key(grad_k_heads)
    proj_grads = jnp.stack(
        [grad_q_flat, grad_k_flat, grad_v_heads.reshape(grad_q_flat.shape)]
    ).astype(jnp.bfloat16)
    grad_qkv = jnp.einsum("sd,tsf->tdf", attn_in, proj_grads, preferred_element_type=jnp.float32)
    grad_attn_in = reduce_rows(
        jnp.einsum("tsf,tdf->sd", proj_grads, w_qkv, preferred_element_type=jnp.float32)
    )
    grad_shift = jnp.sum(grad_attn_in, 0)
    back_one, grad_g_self = pull_self(grad_attn_in)
    grad_one = grad_two + back_one
    grad_first, grad_g_skip = pull_skip(grad_one)
    grad_cols = lax.all_to_all(
        grad_first.astype(jnp.bfloat16), "tensor", split_axis=1, concat_axis=0, tiled=True
    )
    grad_skip_w = multiply_left(joined_full, grad_cols)
    grad_joined = reduce_rows(multiply_right(grad_cols, w_skip))
    model_width = latent_part.shape[-1]
    weight_grads = (
        grad_skip_w,
        grad_qkv,
        grad_out_w,
        grad_cq,
        grad_ckv,
        grad_co,
        grad_up,
        grad_down,
    )
    gain_grads = (
        grad_g_skip,
        grad_g_self,
        grad_g_cross,
        grad_g_mlp,
        grad_g_q,
        grad_g_k,
        grad_g_cq,
        grad_g_ck,
    )
    return (
        output,
        grad_joined[:, :model_width],
        grad_joined[:, model_width:],
        grad_text_part,
        weight_grads,
        gain_grads,
        grad_shift,
    )


def body(
    latent_in,
    skip_in,
    condition,
    text_states,
    positions,
    out_cotangent,
    w_skip,
    w_ada,
    w_qkv,
    w_out,
    w_cq,
    w_ckv,
    w_co,
    w_up,
    w_down,
    g_skip,
    g_self,
    g_cross,
    g_mlp,
    g_q,
    g_k,
    g_cq,
    g_ck,
):
    gain_set = (g_skip, g_self, g_cross, g_mlp, g_q, g_k, g_cq, g_ck)
    micro_count = latent_in.shape[0]
    text_full = lax.all_gather(text_states, "tensor", axis=2, tiled=True)
    silu_cond = jax.nn.silu(condition.astype(jnp.float32)).astype(jnp.bfloat16)
    gathered = None
    outputs, grads_x, grads_skip, grads_text, shift_list = ([], [], [], [], [])
    weight_totals = None
    gain_totals = None
    for micro_index in range(micro_count):
        gathered = (
            lax.all_gather(w_skip, "dp", axis=0, tiled=True),
            lax.all_gather(w_ada, "dp", axis=0, tiled=True),
            lax.all_gather(w_qkv, "dp", axis=1, tiled=True),
            lax.all_gather(w_out, "dp", axis=1, tiled=True),
            lax.all_gather(w_cq, "dp", axis=0, tiled=True),
            lax.all_gather(w_ckv, "dp", axis=1, tiled=True),
            lax.all_gather(w_co, "dp", axis=1, tiled=True),
            lax.all_gather(w_up, "dp", axis=0, tiled=True),
            lax.all_gather(w_down, "dp", axis=1, tiled=True),
        )
        result_set = one_latent(
            gathered,
            gain_set,
            latent_in[micro_index],
            skip_in[micro_index],
            silu_cond[micro_index],
            text_full[micro_index],
            positions[micro_index],
            out_cotangent[micro_index],
        )
        outputs.append(result_set[0])
        grads_x.append(result_set[1])
        grads_skip.append(result_set[2])
        grads_text.append(result_set[3])
        if gain_totals is None:
            gain_totals = result_set[5]
        else:
            gain_totals = jax.tree.map(jnp.add, gain_totals, result_set[5])
        shift_list.append(result_set[6])
        if weight_totals is None:
            weight_totals = result_set[4]
        else:
            weight_totals = jax.tree.map(jnp.add, weight_totals, result_set[4])
    grad_ada = ada_grad(silu_cond, jnp.stack(shift_list))
    shards = send_grads(weight_totals, grad_ada)
    gain_sums = lax.psum(
        (
            gain_totals[0],
            gain_totals[1],
            gain_totals[2],
            gain_totals[3],
            gain_totals[4],
            gain_totals[5],
            gain_totals[6],
            gain_totals[7],
        ),
        ("dp", "tensor"),
    )
    grad_text = lax.psum_scatter(
        jnp.stack(grads_text).astype(jnp.bfloat16), "tensor", scatter_dimension=2, tiled=True
    ).astype(jnp.float32)
    return (
        jnp.stack(outputs),
        jnp.stack(grads_x),
        jnp.stack(grads_skip),
        grad_text,
        shards[0],
        shards[1],
        shards[2],
        shards[3],
        shards[4],
        shards[5],
        shards[6],
        shards[7],
        shards[8],
        gain_sums[0],
        gain_sums[1],
        gain_sums[2],
        gain_sums[3],
        gain_sums[4],
        gain_sums[5],
        gain_sums[6],
        gain_sums[7],
    )


def swap_tensor(values_in):
    return lax.ppermute(values_in, "tensor", [(0, 1), (1, 0)])


def swap_core(values_in):
    count = lax.axis_size("dp")
    return lax.ppermute(values_in, "dp", [(i, i ^ 1) for i in range(count)])


def join_pair(own, other, index, axis):
    return jnp.concatenate(
        [jnp.where(index == 0, own, other), jnp.where(index == 0, other, own)], axis
    )


def choose(values_in, index, axis=0):
    return lax.dynamic_index_in_dim(values_in, index, axis, keepdims=False)


def whole_attend(queries, key_vecs, values, scale_factor):
    scores = (
        jnp.einsum("qhd,khd->hqk", queries, key_vecs, preferred_element_type=jnp.float32)
        * scale_factor
    )
    row_max = jnp.max(scores, -1, keepdims=True)
    weights = jnp.exp(scores - row_max)
    row_total = jnp.sum(weights, -1, keepdims=True)
    probs_low = (weights / row_total).astype(jnp.bfloat16)
    mixed_out = jnp.einsum("hqk,khd->qhd", probs_low, values, preferred_element_type=jnp.float32)
    return (mixed_out.astype(jnp.bfloat16), row_max + jnp.log(row_total))


def whole_attend_back(queries, key_vecs, values, log_sums, grad_mixed, scale_factor):
    scores = (
        jnp.einsum("qhd,khd->hqk", queries, key_vecs, preferred_element_type=jnp.float32)
        * scale_factor
    )
    probs = jnp.exp(scores - log_sums)
    grad_probs = jnp.einsum("qhd,khd->hqk", grad_mixed, values, preferred_element_type=jnp.float32)
    delta_row = jnp.sum(grad_probs * probs, -1, keepdims=True)
    grad_scores = (probs * (grad_probs - delta_row)).astype(jnp.bfloat16)
    grad_query = (
        jnp.einsum("hqk,khd->qhd", grad_scores, key_vecs, preferred_element_type=jnp.float32)
        * scale_factor
    )
    grad_keys = (
        jnp.einsum("hqk,qhd->khd", grad_scores, queries, preferred_element_type=jnp.float32)
        * scale_factor
    )
    grad_values = jnp.einsum(
        "hqk,qhd->khd", probs.astype(jnp.bfloat16), grad_mixed, preferred_element_type=jnp.float32
    )
    return (grad_query, grad_keys, grad_values)


def pair_body(
    latent_in,
    skip_in,
    condition,
    text_states,
    positions,
    out_cotangent,
    w_skip,
    w_ada,
    w_qkv,
    w_out,
    w_cq,
    w_ckv,
    w_co,
    w_up,
    w_down,
    g_skip,
    g_self,
    g_cross,
    g_mlp,
    g_q,
    g_k,
    g_cq,
    g_ck,
):
    low = jnp.bfloat16
    dp_count = lax.axis_size("dp")
    dp_index = lax.axis_index("dp")
    side = lax.axis_index("tensor")
    core = lax.rem(dp_index, 2)
    groups = [list(range(c, dp_count, 2)) for c in range(2)]
    width = latent_in.shape[-1]
    head_size = g_q.shape[0]
    scale_factor = head_size ** (-0.5)

    def take_tokens(values_in):
        got = swap_tensor(choose(values_in, 1 - side))
        return join_pair(choose(values_in, side), got, side, 0)

    def give_tokens(values_in, kind):
        halves = values_in.reshape(2, values_in.shape[0] // 2, values_in.shape[1])
        got = swap_tensor(choose(halves, 1 - side).astype(low)).astype(kind)
        own = choose(halves, side).astype(kind)
        return jnp.stack([jnp.where(side == 0, own, got), jnp.where(side == 0, got, own)])

    def whole_weight(shard):
        rows = shard.shape[0]
        joined = join_pair(shard, swap_tensor(shard), side, shard.ndim - 1)
        return lax.all_gather(joined.reshape(rows, -1), "dp", axis=0, tiled=True)

    latent_own = take_tokens(latent_in)
    skip_own = take_tokens(skip_in)
    full_skip = whole_weight(w_skip)
    silu_all = jax.nn.silu(
        lax.all_gather(condition, "dp", axis=0, tiled=True).astype(jnp.float32)
    ).astype(low)
    ada_rows = w_ada.shape[0]
    silu_cols = lax.dynamic_slice_in_dim(silu_all, dp_index * ada_rows, ada_rows, 1)
    shift_vec = choose(
        lax.psum_scatter(multiply(silu_cols, w_ada), "dp", scatter_dimension=0, tiled=True), side
    )
    full_qkv = whole_weight(w_qkv.transpose(1, 0, 2))
    full_out = whole_weight(w_out.T)
    full_cq = whole_weight(w_cq)
    full_ckv = whole_weight(w_ckv.transpose(1, 0, 2))
    full_co = whole_weight(w_co.T)
    full_up = whole_weight(w_up)
    full_down = whole_weight(w_down.T)
    text_got = swap_tensor(choose(text_states, 1 - side))
    text_own = join_pair(choose(text_states, side), text_got, side, 1)
    grad_top = take_tokens(out_cotangent)
    cosine, sine_tab = rope_tables(choose(positions, side), head_size)

    def rotary(flat_in, gain_vec):
        split_in = flat_in.reshape(flat_in.shape[0], -1, head_size)
        normed = layer_norm(split_in, gain_vec)
        return normed * cosine[:, None, :] + rotate_half(normed) * sine_tab[:, None, :]

    def head_norm(flat_in, gain_vec):
        return layer_norm(flat_in.reshape(flat_in.shape[0], -1, head_size), gain_vec)

    def grad_shard(left_side, right_side, parts):
        half = right_side.shape[1] // 2
        there = multiply_left(
            left_side, lax.dynamic_slice_in_dim(right_side, (1 - core) * half, half, 1)
        ).astype(low)
        here = multiply_left(left_side, lax.dynamic_slice_in_dim(right_side, core * half, half, 1))
        chip_sum = (here + swap_core(there).astype(jnp.float32)).astype(low)
        part = lax.psum_scatter(
            chip_sum, "dp", scatter_dimension=0, axis_index_groups=groups, tiled=True
        )
        rows = part.shape[0] // 2
        part = part.reshape(2, rows, half)
        got = swap_core(choose(part, 1 - core))
        joined = join_pair(choose(part, core), got, core, 1).reshape(rows, parts, 2, -1)
        got = swap_tensor(choose(joined, 1 - side, 2))
        return choose(joined, side, 2).astype(jnp.float32) + got.astype(jnp.float32)

    joined_full = jnp.concatenate([latent_own, skip_own], -1)
    first_out = multiply(joined_full, full_skip).astype(low).astype(jnp.float32)
    resid_one, pull_skip = jax.vjp(layer_norm, first_out, g_skip)
    normed_self, pull_self = jax.vjp(layer_norm, resid_one, g_self)
    attn_in = (normed_self + shift_vec).astype(low)
    projected = multiply(attn_in, full_qkv)
    query_rot, pull_query = jax.vjp(rotary, projected[:, :width], g_q)
    key_rot, pull_key = jax.vjp(rotary, projected[:, width : 2 * width], g_k)
    queries = query_rot.astype(low)
    key_vecs = key_rot.astype(low)
    values = projected[:, 2 * width :].astype(low).reshape(queries.shape)
    mixed_out, log_sums = whole_attend(queries, key_vecs, values, scale_factor)
    mixed_flat = mixed_out.reshape(mixed_out.shape[0], -1)
    resid_two = resid_one + multiply_right(mixed_flat, full_out)
    normed_cross, pull_cross = jax.vjp(layer_norm, resid_two, g_cross)
    cross_in = normed_cross.astype(low)
    cross_query_rot, pull_cross_query = jax.vjp(rotary, multiply(cross_in, full_cq), g_cq)
    text_proj = multiply(text_own, full_ckv)
    cross_key_rot, pull_cross_key = jax.vjp(head_norm, text_proj[:, :width], g_ck)
    cross_queries = cross_query_rot.astype(low)
    cross_keys = cross_key_rot.astype(low)
    cross_values = text_proj[:, width:].astype(low).reshape(cross_keys.shape)
    cross_mixed, cross_sums = whole_attend(cross_queries, cross_keys, cross_values, scale_factor)
    cross_flat = cross_mixed.reshape(cross_mixed.shape[0], -1)
    resid_three = resid_two + multiply_right(cross_flat, full_co)
    normed_mlp, pull_mlp = jax.vjp(layer_norm, resid_three, g_mlp)
    mlp_in = normed_mlp.astype(low)
    inner_pre = multiply(mlp_in, full_up)
    hidden_val, pull_gelu = jax.vjp(gelu_tanh, inner_pre)
    hidden_low = hidden_val.astype(low)
    resid_four = resid_three + multiply_right(hidden_low, full_down)
    output = give_tokens(resid_four, low)

    grad_four = grad_top.astype(jnp.float32)
    shard_down = grad_shard(grad_top, hidden_low, 1)
    grad_hidden = multiply(grad_top, full_down).astype(low).astype(jnp.float32)
    (grad_inner,) = pull_gelu(grad_hidden)
    grad_inner_low = grad_inner.astype(low)
    shard_up = grad_shard(mlp_in, grad_inner_low, 1)
    back_three, grad_g_mlp = pull_mlp(multiply_right(grad_inner_low, full_up))
    grad_three = grad_four + back_three
    grad_cross_out = grad_three.astype(low)
    shard_co = grad_shard(grad_cross_out, cross_flat, 1)
    grad_cross_mixed = multiply(grad_cross_out, full_co).astype(low).reshape(cross_mixed.shape)
    grad_cq_heads, grad_ck_heads, grad_cv_heads = whole_attend_back(
        cross_queries, cross_keys, cross_values, cross_sums, grad_cross_mixed, scale_factor
    )
    grad_cq_flat, grad_g_cq = pull_cross_query(grad_cq_heads)
    grad_ck_flat, grad_g_ck = pull_cross_key(grad_ck_heads)
    grad_cq_low = grad_cq_flat.astype(low)
    text_grads_low = jnp.concatenate(
        [grad_ck_flat, grad_cv_heads.reshape(grad_ck_flat.shape)], -1
    ).astype(low)
    shard_cq = grad_shard(cross_in, grad_cq_low, 1)
    shard_ckv = grad_shard(text_own, text_grads_low, 2)
    grad_text_own = multiply_right(text_grads_low, full_ckv)
    text_cols = grad_text_own.reshape(grad_text_own.shape[0], 2, -1)
    text_kept = choose(text_cols, side, 1)
    text_got = swap_tensor(choose(text_cols, 1 - side, 1).astype(low)).astype(jnp.float32)
    grad_text = jnp.stack(
        [jnp.where(side == 0, text_kept, text_got), jnp.where(side == 0, text_got, text_kept)]
    )
    back_two, grad_g_cross = pull_cross(multiply_right(grad_cq_low, full_cq))
    grad_two = grad_three + back_two
    grad_self_out = grad_two.astype(low)
    shard_out = grad_shard(grad_self_out, mixed_flat, 1)
    grad_mixed = multiply(grad_self_out, full_out).astype(low).reshape(mixed_out.shape)
    grad_q_heads, grad_k_heads, grad_v_heads = whole_attend_back(
        queries, key_vecs, values, log_sums, grad_mixed, scale_factor
    )
    grad_q_flat, grad_g_q = pull_query(grad_q_heads)
    grad_k_flat, grad_g_k = pull_key(grad_k_heads)
    proj_grads = jnp.concatenate(
        [grad_q_flat, grad_k_flat, grad_v_heads.reshape(grad_q_flat.shape)], -1
    ).astype(low)
    shard_qkv = grad_shard(attn_in, proj_grads, 3)
    grad_attn_in = multiply_right(proj_grads, full_qkv)
    grad_shift = jnp.sum(grad_attn_in, 0)
    back_one, grad_g_self = pull_self(grad_attn_in)
    grad_one = grad_two + back_one
    grad_first, grad_g_skip = pull_skip(grad_one)
    grad_first_low = grad_first.astype(low)
    shard_skip = grad_shard(joined_full, grad_first_low, 1)
    grad_joined = multiply_right(grad_first_low, full_skip)
    grad_x = give_tokens(grad_joined[:, :width], jnp.float32)
    grad_skip = give_tokens(grad_joined[:, width:], jnp.float32)

    shift_all = lax.all_gather(grad_shift[None, :], ("dp", "tensor"), axis=0, tiled=True)
    grad_ada = lax.dot_general(
        silu_cols.astype(jnp.float32), shift_all, (((0,), (0,)), ((), ())), precision=HIGH
    )
    gain_list = (
        grad_g_skip,
        grad_g_self,
        grad_g_cross,
        grad_g_mlp,
        grad_g_q,
        grad_g_k,
        grad_g_cq,
        grad_g_ck,
    )
    gain_total = lax.psum(jnp.concatenate(gain_list), ("dp", "tensor"))
    gain_sums, place = [], 0
    for gain in gain_list:
        gain_sums.append(gain_total[place : place + gain.shape[0]])
        place += gain.shape[0]

    def flat(shard):
        return shard.reshape(shard.shape[0], -1)

    return (
        output,
        grad_x,
        grad_skip,
        grad_text,
        flat(shard_skip),
        grad_ada,
        shard_qkv.transpose(1, 0, 2),
        flat(shard_out).T,
        flat(shard_cq),
        shard_ckv.transpose(1, 0, 2),
        flat(shard_co).T,
        flat(shard_up),
        flat(shard_down).T,
        *gain_sums,
    )


def pick_body(mesh):
    def chosen(*arrays):
        pair = mesh.shape["tensor"] == 2 and arrays[0].shape[0] == 2 and mesh.shape["dp"] % 2 == 0
        return (pair_body if pair else body)(*arrays)

    return chosen


def solution(mesh):
    return jax.shard_map(
        pick_body(mesh),
        mesh=mesh,
        in_specs=(
            P("dp", "tensor", None),
            P("dp", "tensor", None),
            P("dp", None),
            P("dp", None, "tensor"),
            P("dp", None, None),
            P("dp", "tensor", None),
            P("dp", "tensor"),
            P("dp", None),
            P(None, "dp", "tensor"),
            P("tensor", "dp"),
            P("dp", "tensor"),
            P(None, "dp", "tensor"),
            P("tensor", "dp"),
            P("dp", "tensor"),
            P("tensor", "dp"),
            P(),
            P(),
            P(),
            P(),
            P(),
            P(),
            P(),
            P(),
        ),
        out_specs=(
            P("dp", "tensor", None),
            P("dp", "tensor", None),
            P("dp", "tensor", None),
            P("dp", None, "tensor"),
            P("dp", "tensor"),
            P("dp", None),
            P(None, "dp", "tensor"),
            P("tensor", "dp"),
            P("dp", "tensor"),
            P(None, "dp", "tensor"),
            P("tensor", "dp"),
            P("dp", "tensor"),
            P("tensor", "dp"),
            P(),
            P(),
            P(),
            P(),
            P(),
            P(),
            P(),
            P(),
        ),
        check_vma=False,
    )
```
